32 devices in a mesh: row: 4 (over y, x), col: 8 (over z, core).
Axes of the slice: x: 2, y: 2, z: 4, core: 2. Of those that a mesh axis runs over, the one named last changes fastest.
Arguments:
- panel_right: bfloat16 [32, 1536, 128], P('row', 'col'), may hold values from -1 to 1
- factor_inverse: bfloat16 [1536, 1536], replicated, as said below
- ranks: int32 [32], P(('row', 'col')), may hold values from 32 to 128
- owner_map: int32 [32], replicated, may hold values from 0 to 31, each once
- cores: float32 [4, 8, 8, 4, 128, 128], P('row', 'col'), may hold values from -6 to 6
Outputs:
- new_cores: float32 [4, 8, 8, 4, 128, 128], P('row', 'col')
The draws below stay inside these ranges and needn't reach their ends.
Inputs may be any that keep to these rules, and one draw needn't show every extreme that they name: `factor_inverse`: lower triangular, the inverse of a Cholesky factor.
All inputs are finite; a program needn't handle non-finite values.
Results may differ from the reference program's by a relative error of at most 0.0033.
Values may be sent and summed in bfloat16 or wider, within the bound.
No kernel may reach another device: no remote copies, remote signals or barrier semaphores. Data moves between devices by JAX's collectives and lax.ppermute only.
A program may use at most 128 MiB of HBM per device.

```python
import jax
import jax.numpy as jnp
from jax import lax

B = 1536
R = 128
NP = 32
N_ROW = 4
N_COL = 8


def draw_factor_inverse(key, part):
    first, second = jax.random.split(key)
    spread = jax.random.normal(first, (B, B), jnp.float32)
    lower = jnp.tril(spread * (0.5 / B ** 0.5), -1)
    diagonal = jax.random.uniform(second, (B,), jnp.float32, 1.0, 2.0)
    return (lower + jnp.diag(diagonal)).astype(jnp.bfloat16)


def touch_ends(drawn, stream_key, least, largest):
    longest = drawn.shape.index(max(drawn.shape))
    spots = []
    for shift in (0, 1):
        where = [jax.random.randint(jax.random.fold_in(stream_key, axis), (), 0, length) for axis, length in enumerate(drawn.shape)]
        where[longest] = (where[longest] + shift) % drawn.shape[longest]
        spots.append(tuple(where))
    return drawn.at[spots[0]].set(least).at[spots[1]].set(largest)


def block_scale(stream_key, extent, cuts, smallest, top_value):
    factor_of = 1.0
    for position, blocks in cuts:
        draws = jax.random.uniform(jax.random.fold_in(jax.random.fold_in(stream_key, 6), position), (blocks,), jnp.float32, smallest / len(cuts), top_value / len(cuts))
        factor_of = factor_of * jnp.repeat(jnp.exp(draws), extent[position] // blocks).reshape((-1,) + (1,) * (len(extent) - 1 - position))
    return factor_of


def scatter_about(rng, extent, scale, most, cuts=(), kind=jnp.bfloat16):
    entries = jax.random.normal(rng, extent, jnp.float32) * scale
    if len(cuts) > 0:
        entries = block_scale(rng, extent, cuts, -0.22, 0.18) * entries
    return jnp.clip(entries, min=-most, max=most).astype(kind)


def setup_inputs(seed: int = 0) -> dict:
    splits = jax.random.split(jax.random.key(seed), 6)
    return {
        "panel_right": scatter_about(splits[0], (NP, B, R), 0.16, 1.0, ((0, 4), (1, 8))),
        "factor_inverse": draw_factor_inverse(jax.random.fold_in(splits[5], 71), 0),
        "ranks": touch_ends(jax.random.randint(splits[2], (NP,), R // 4, R + 1), jax.random.fold_in(splits[2], 1), R // 4, R).astype(jnp.int32),
        "owner_map": jax.random.permutation(splits[3], NP).astype(jnp.int32),
        "cores": scatter_about(splits[4], (N_ROW, N_COL, N_COL, N_ROW, R, R), 1.0, 6.0, ((0, 4), (1, 8)), jnp.float32),
    }


def reference(panel_right, factor_inverse, ranks, owner_map, cores):
    solved = jnp.einsum("ij,pjk->pik", factor_inverse.astype(jnp.float32), panel_right.astype(jnp.float32))
    column = lax.broadcasted_iota(jnp.int32, (1, 1, R), 2)
    keep = column < ranks.reshape(NP, 1, 1)
    panel_left = jnp.where(keep, solved, 0.0).astype(jnp.bfloat16)
    grid_map = owner_map.reshape(N_ROW, N_COL)
    right_side = panel_left[grid_map.reshape(NP)].reshape(N_ROW, N_COL, B, R).astype(jnp.float32)

    def one_row(row_index):
        lefts = panel_left[grid_map[row_index]].astype(jnp.float32)
        gram = jnp.einsum("aik,bcil->cabkl", lefts, right_side)
        return cores[row_index] - gram

    return lax.map(one_row, jnp.arange(N_ROW, dtype=jnp.int32))
```

```python
import functools

import jax
import jax.numpy as jnp
from jax import lax
from jax.experimental import pallas as pl
from jax.experimental.pallas import tpu as pltpu
from jax.sharding import PartitionSpec as P

VMEM = pl.BlockSpec(memory_space=pltpu.VMEM)
SMEM = pl.BlockSpec(memory_space=pltpu.SMEM)
ANY = pl.BlockSpec(memory_space=pl.ANY)


def room(mebibytes):
    return pltpu.CompilerParams(vmem_limit_bytes=mebibytes << 20)


def near(value):
    return pltpu.with_memory_space_constraint(value, pltpu.VMEM)


def swap(value, axis, mask):
    count = lax.axis_size(axis)
    return lax.ppermute(value, axis, [(i, i ^ mask) for i in range(count)])


def hypercube(value, axis, count, stride):
    held = [value] + [None] * (count - 1)
    for q in sorted(range(1, count), key=lambda n: (bin(n).count("1"), -n)):
        low = q & -q
        held[q] = swap(held[q ^ low], axis, low * stride)
    return held


def split_kernel(count, place_ref, rank_ref, x_ref, *outs):
    row, blocks = place_ref[0], x_ref.shape[0]
    rank = jnp.full(outs[0].shape[1:], rank_ref[0], jnp.float32).astype(x_ref.dtype)
    for m in range(count):
        outs[m][:blocks] = x_ref[:, row ^ m]
        outs[m][blocks] = rank


def split_rows(place, ranks, x):
    blocks, count, piece, width = x.shape
    return pl.pallas_call(
        functools.partial(split_kernel, count),
        out_shape=[pltpu.VMEM((blocks + 1, piece, width), x.dtype)] * count,
        in_specs=[SMEM, SMEM, VMEM],
        out_specs=[VMEM] * count,
        compiler_params=room(8),
    )(place, ranks, near(x))


def reorder_kernel(n_row, n_col, place_ref, map_ref, *refs):
    pieces, row_outs = refs[:n_row], refs[n_row : 2 * n_row]
    col_outs, rank_out, held = refs[2 * n_row : -2], refs[-2], refs[-1]
    row, col = place_ref[0], place_ref[1]
    rank_out[...] = jnp.zeros_like(rank_out)
    for m in range(n_row):
        held[m * n_col : (m + 1) * n_col] = pieces[m][:n_col]
        rank_out[0, m : m + 1] = pieces[m][n_col, m : m + 1]

    def block(grid_index):
        owner = map_ref[grid_index]
        return held[((owner // n_col) ^ row) * n_col + owner % n_col]

    for m in range(n_row):
        for a in range(n_col):
            row_outs[m][a] = block((row ^ m) * n_col + a)
    for q in range(n_col // 2):
        for j in range(2):
            for b in range(n_row):
                col_outs[q][j, b] = block(b * n_col + (col ^ (2 * q + j)))


def reorder(place, owner_map, pieces, n_row, n_col):
    _, piece, width = pieces[0].shape
    dtype = pieces[0].dtype
    outs = pl.pallas_call(
        functools.partial(reorder_kernel, n_row, n_col),
        out_shape=[pltpu.VMEM((n_col, piece, width), dtype)] * n_row
        + [pltpu.VMEM((2, n_row, piece, width), dtype)] * (n_col // 2)
        + [pltpu.VMEM((1, piece, width), dtype)],
        in_specs=[SMEM, SMEM] + [VMEM] * n_row,
        out_specs=[VMEM] * (n_row + n_col // 2 + 1),
        scratch_shapes=[pltpu.VMEM((n_row * n_col, piece, width), dtype)],
        compiler_params=room(8),
    )(place, owner_map, *map(near, pieces))
    return outs[:n_row], outs[n_row:-1], outs[-1]


def solve_kernel(n_row, n_col, piece, step, place_ref, factor_ref, turned_ref, *refs):
    parts, out, whole = refs[:-2], refs[-2], refs[-1]
    row, col = place_ref[0], place_ref[1]
    width = parts[0].shape[-1]
    order = factor_ref.shape[0]
    if len(parts) == 1:
        whole[...] = parts[0][...]
    else:
        for m in range(n_row):
            for j in range(2):
                for q in range(n_col // 2):
                    start = ((col ^ (2 * q + j)) * n_row + (row ^ m)) * piece
                    rows = pl.ds(pl.multiple_of(start, piece), piece)
                    for b in range(n_row):
                        whole[rows, b * width : (b + 1) * width] = parts[m][j, q, b]
    for top in reversed(range(0, order, step)):
        end = top + step
        left = jnp.dot(factor_ref[top:end, :end], whole[:end], preferred_element_type=jnp.float32)
        whole[top:end] = left.astype(whole.dtype)
    for top in range(0, order, step):
        end = top + step
        both = jnp.dot(turned_ref[top:end, top:], whole[top:], preferred_element_type=jnp.float32)
        out[top:end] = both.astype(out.dtype)


def solve(place, factor, turned, parts, n_row, n_col, piece):
    order, width = factor.shape[0], parts[0].shape[-1]
    step = 256 if order % 256 == 0 else order
    if piece % 16:
        stacked = jnp.stack(parts).reshape(n_row, n_col, n_row, piece, width)
        col, row = jnp.arange(n_col)[:, None] ^ place[1], jnp.arange(n_row)[None] ^ place[0]
        parts = stacked[row, (col % 2) * (n_col // 2) + col // 2]
        parts = [parts.transpose(0, 1, 3, 2, 4).reshape(order, n_row * width)]
    return pl.pallas_call(
        functools.partial(solve_kernel, n_row, n_col, piece, step),
        out_shape=pltpu.VMEM((order, n_row * width), factor.dtype),
        in_specs=[SMEM, VMEM, VMEM] + [VMEM] * len(parts),
        out_specs=VMEM,
        scratch_shapes=[pltpu.VMEM((order, n_row * width), factor.dtype)],
        compiler_params=room(24),
    )(place, factor, turned, *map(near, parts))


def strip(ref, a, n_row, n_col):
    if ref.shape[0] == n_col:
        return ref[a]
    return jnp.concatenate([ref[n * n_col + a] for n in range(n_row)], axis=0)


def gram_of(n_row, n_col, a, strips, turned):
    left = jnp.concatenate([strip(ref, a, n_row, n_col) for ref in strips], axis=0)
    return lax.dot_general(
        left, turned[...], (((0,), (0,)), ((), ())), preferred_element_type=jnp.float32
    )


def turn_rows(n_row, n_col, piece, masks, place_ref, both_ref, turned):
    if piece % 16:
        turned[...] = both_ref[...]
        return
    row, col = place_ref[0], place_ref[1]
    for i, m in enumerate(masks):
        for n in range(n_row):
            start = ((col ^ m) * n_row + (row ^ n)) * piece
            rows = pl.ds(pl.multiple_of(start, piece), piece)
            there = (i * n_row + n) * piece
            turned[there : there + piece] = both_ref[rows]


def gram_first_kernel(n_row, n_col, piece, masks, place_ref, both_ref, *refs):
    strips, out, turned = refs[:-2], refs[-2], refs[-1]
    turn_rows(n_row, n_col, piece, masks, place_ref, both_ref, turned)
    for a in range(n_col):
        out[a] = gram_of(n_row, n_col, a, strips, turned)


def gram_last_kernel(n_row, n_col, piece, masks, place_ref, map_ref, both_ref, first_ref, cores_ref, *refs):
    strips, chunks = refs[: len(masks)], refs[len(masks) : len(masks) + n_col]
    out, turned, table = refs[-3:]
    row, col = place_ref[0], place_ref[1]
    width = cores_ref.shape[-1]
    turn_rows(n_row, n_col, piece, masks, place_ref, both_ref, turned)
    for m in range(n_col):
        for n in range(n_row):
            rank = chunks[m][n_row * n_col, n : n + 1].astype(jnp.float32)
            table[m * n_row + n] = jnp.broadcast_to(rank, table.shape[1:])
    down = lax.broadcasted_iota(jnp.int32, (width, width), 0).astype(jnp.float32)
    across = lax.broadcasted_iota(jnp.int32, (width, width), 1).astype(jnp.float32)

    def rank_of(grid_index):
        owner = map_ref[grid_index]
        entry = ((owner % n_col) ^ col) * n_row + ((owner // n_col) ^ row)
        return table[entry][:1]

    for a in range(n_col):
        gram = gram_of(n_row, n_col, a, strips, turned) + first_ref[a]
        deep = down < rank_of(row * n_col + a)
        for b in range(n_row):
            keep = deep & (across < rank_of(b * n_col + col))
            tile = gram[:, b * width : (b + 1) * width]
            out[a, b] = cores_ref[a, b] - jnp.where(keep, tile, 0.0)


def gram_update(place, owner_map, both, cores, chunks, n_row, n_col, piece):
    order, total = both.shape
    width = cores.shape[-1]
    strips = chunks
    whole = both.reshape(n_col, n_row, piece, total)
    if piece % 16:
        strips = [
            chunk[:-1].reshape(n_row, n_col, piece, width).transpose(1, 0, 2, 3).reshape(n_col, -1, width)
            for chunk in chunks
        ]

    def rows_for(masks):
        if piece % 16 == 0:
            return both
        there = jnp.asarray(masks)[:, None] ^ place[1], jnp.arange(n_row)[None] ^ place[0]
        return whole[there].reshape(-1, total)

    cut = n_col - 2
    height = order // n_col
    first = pl.pallas_call(
        functools.partial(gram_first_kernel, n_row, n_col, piece, tuple(range(cut))),
        out_shape=pltpu.VMEM((n_col, width, total), jnp.float32),
        in_specs=[SMEM, VMEM] + [VMEM] * cut,
        out_specs=VMEM,
        scratch_shapes=[pltpu.VMEM((cut * height, total), both.dtype)],
        compiler_params=room(16),
    )(place, near(rows_for(range(cut))), *map(near, strips[:cut]))
    return pl.pallas_call(
        functools.partial(gram_last_kernel, n_row, n_col, piece, tuple(range(cut, n_col))),
        out_shape=jax.ShapeDtypeStruct(cores.shape, cores.dtype),
        in_specs=[SMEM, SMEM] + [VMEM] * (3 + n_col - cut + n_col),
        out_specs=VMEM,
        scratch_shapes=[
            pltpu.VMEM(((n_col - cut) * height, total), both.dtype),
            pltpu.VMEM((n_row * n_col, 8, width), jnp.float32),
        ],
        compiler_params=room(24),
    )(place, owner_map, near(rows_for(range(cut, n_col))), near(first), cores, *map(near, strips[cut:]), *map(near, chunks))


def body(panel_right, factor_inverse, ranks, owner_map, cores):
    n_row = lax.axis_size("row")
    n_col = lax.axis_size("col")
    blocks, rows, width = panel_right.shape
    piece = rows // n_row
    row = lax.axis_index("row")
    col = lax.axis_index("col")
    place = jnp.stack([row, col]).astype(jnp.int32)
    planes = n_col // 2

    parts = split_rows(place, ranks, panel_right.reshape(blocks, n_row, piece, width))
    parts = [parts[0]] + [swap(parts[m], "row", m) for m in range(1, n_row)]
    row_parts, col_parts, rank_rows = reorder(place, owner_map, parts, n_row, n_col)

    col_parts = [col_parts[0]] + [swap(col_parts[q], "col", 2 * q) for q in range(1, planes)]
    row_parts = [row_parts[0]] + [swap(row_parts[m], "row", m) for m in range(1, n_row)]
    mine = jnp.stack([part[0] for part in col_parts])
    theirs = swap(jnp.stack([part[1] for part in col_parts]), "col", 1)
    col_set = hypercube(jnp.stack([mine, theirs]), "row", n_row, 1)
    row_set = hypercube(jnp.concatenate(row_parts + [rank_rows]), "col", planes, 2)
    chunks = []
    for part in row_set:
        chunks += [part, swap(part, "col", 1)]

    turned = lax.optimization_barrier(factor_inverse.T)
    both = solve(place, factor_inverse, turned, col_set, n_row, n_col, piece)
    return gram_update(place, owner_map, both, cores[0, 0], chunks, n_row, n_col, piece)[None, None]


def solution(mesh):
    return jax.shard_map(
        body,
        mesh=mesh,
        in_specs=(
            P("row", "col", None),
            P(),
            P(("row", "col")),
            P(),
            P("row", "col", None, None, None, None),
        ),
        out_specs=P("row", "col", None, None, None, None),
        check_vma=False,
    )
```

```python
import functools

import jax
import jax.numpy as jnp
from jax import lax
from jax.experimental import pallas as pl
from jax.experimental.pallas import tpu as pltpu
from jax.sharding import PartitionSpec as P


VMEM = pl.BlockSpec(memory_space=pltpu.VMEM)
SMEM = pl.BlockSpec(memory_space=pltpu.SMEM)
HBM = pl.BlockSpec(memory_space=pltpu.HBM)


def room(mebibytes):
    return pltpu.CompilerParams(vmem_limit_bytes=mebibytes << 20)


def near(value):
    return pltpu.with_memory_space_constraint(value, pltpu.VMEM)


def swap(value, axis, mask):
    count = lax.axis_size(axis)
    return lax.ppermute(value, axis, [(i, i ^ mask) for i in range(count)])


def hops(count):
    return sorted(range(1, count), key=lambda n: (bin(n).count("1"), -n))


def hypercube(value, axis, count, stride):
    held = [value] + [None] * (count - 1)
    for q in hops(count):
        low = q & -q
        held[q] = swap(held[q ^ low], axis, low * stride)
    return held


def two_way_hypercube(value, axis, count):
    held = [value] + [None] * (count - 1)
    for m in hops(count):
        low, high = m & -m, 1 << (m.bit_length() - 1)
        if low == high:
            held[m] = swap(value, axis, m)
            continue
        half = value.shape[0] // 2
        first = swap(held[m ^ low][:half], axis, low)
        second = swap(held[m ^ high][half:], axis, high)
        held[m] = jnp.concatenate([first, second])
    return held


def split_kernel(count, place_ref, rank_ref, map_ref, x_ref, *refs):
    outs, map_out, sem = refs[:count], refs[count], refs[count + 1]
    row, blocks = place_ref[0], x_ref.shape[0]
    copies = [
        pltpu.make_async_copy(x_ref.at[:, row ^ m], outs[m].at[:blocks], sem.at[m])
        for m in range(count)
    ]
    for copy in copies:
        copy.start()
    rank = jnp.full(outs[0].shape[1:], rank_ref[0], jnp.float32).astype(x_ref.dtype)
    for m in range(count):
        outs[m][blocks] = rank
    for g in range(map_out.shape[0]):
        map_out[g] = map_ref[g]
    for copy in copies:
        copy.wait()


def split_rows(place, ranks, owner_map, x):
    blocks, count, piece, width = x.shape
    return pl.pallas_call(
        functools.partial(split_kernel, count),
        out_shape=[pltpu.VMEM((blocks + 1, piece, width), x.dtype)] * count
        + [pltpu.SMEM(owner_map.shape, owner_map.dtype)],
        in_specs=[SMEM, SMEM, SMEM, HBM],
        out_specs=[VMEM] * count + [SMEM],
        scratch_shapes=[pltpu.SemaphoreType.DMA((count,))],
        compiler_params=room(8),
    )(place, ranks, owner_map, x)


def fetch_kernel(step, factor_ref, near_ref, turned_ref, sem):
    copy = pltpu.make_async_copy(factor_ref, near_ref, sem)
    copy.start()
    copy.wait()
    order = near_ref.shape[0]
    for top in range(0, order, step):
        for left in range(0, top + step, step):
            block = near_ref[top : top + step, left : left + step]
            turned_ref[left : left + step, top : top + step] = block.T


def fetch(factor, step):
    return pl.pallas_call(
        functools.partial(fetch_kernel, step),
        out_shape=[pltpu.VMEM(factor.shape, factor.dtype)] * 2,
        in_specs=[HBM],
        out_specs=[VMEM] * 2,
        scratch_shapes=[pltpu.SemaphoreType.DMA],
        compiler_params=room(16),
    )(factor)


def reorder_kernel(n_row, n_col, place_ref, map_ref, *refs):
    pieces, row_outs = refs[:n_row], refs[n_row : 2 * n_row]
    col_outs, rank_out, held = refs[2 * n_row : -2], refs[-2], refs[-1]
    row, col = place_ref[0], place_ref[1]
    rank_out[...] = jnp.zeros_like(rank_out)
    for m in range(n_row):
        held[m * n_col : (m + 1) * n_col] = pieces[m][:n_col]
        rank_out[0, m : m + 1] = pieces[m][n_col, m : m + 1]

    def block(grid_index):
        owner = map_ref[grid_index]
        return held[((owner // n_col) ^ row) * n_col + owner % n_col]

    for m in range(n_row):
        for a in range(n_col):
            row_outs[m][a] = block((row ^ m) * n_col + a)
    for q in range(n_col // 2):
        for j in range(2):
            for b in range(n_row):
                col_outs[q][j, b] = block(b * n_col + (col ^ (2 * q + j)))


def reorder(place, owner_map, pieces, n_row, n_col):
    _, piece, width = pieces[0].shape
    dtype = pieces[0].dtype
    outs = pl.pallas_call(
        functools.partial(reorder_kernel, n_row, n_col),
        out_shape=[pltpu.VMEM((n_col, piece, width), dtype)] * n_row
        + [pltpu.VMEM((2, n_row, piece, width), dtype)] * (n_col // 2)
        + [pltpu.VMEM((1, piece, width), dtype)],
        in_specs=[SMEM, SMEM] + [VMEM] * n_row,
        out_specs=[VMEM] * (n_row + n_col // 2 + 1),
        scratch_shapes=[pltpu.VMEM((n_row * n_col, piece, width), dtype)],
        compiler_params=room(8),
    )(place, owner_map, *map(near, pieces))
    return outs[:n_row], outs[n_row:-1], outs[-1]


def solve_kernel(n_row, n_col, piece, step, place_ref, factor_ref, turned_ref, *refs):
    parts, out, whole = refs[:-2], refs[-2], refs[-1]
    row, col = place_ref[0], place_ref[1]
    width = parts[0].shape[-1]
    order = factor_ref.shape[0]
    if len(parts) == 1:
        whole[...] = parts[0][...]
    else:
        for m in range(n_row):
            for j in range(2):
                for q in range(n_col // 2):
                    start = ((col ^ (2 * q + j)) * n_row + (row ^ m)) * piece
                    rows = pl.ds(pl.multiple_of(start, piece), piece)
                    for b in range(n_row):
                        whole[rows, b * width : (b + 1) * width] = parts[m][j, q, b]
    for top in reversed(range(0, order, step)):
        end = top + step
        left = jnp.dot(factor_ref[top:end, :end], whole[:end], preferred_element_type=jnp.float32)
        whole[top:end] = left.astype(whole.dtype)
    for top in range(0, order, step):
        end = top + step
        both = jnp.dot(turned_ref[top:end, top:], whole[top:], preferred_element_type=jnp.float32)
        out[top:end] = both.astype(out.dtype)


def solve(place, factor, turned, parts, n_row, n_col, piece, step):
    order, width = factor.shape[0], parts[0].shape[-1]
    if piece % 16:
        stacked = jnp.stack(parts).reshape(n_row, n_col, n_row, piece, width)
        col, row = jnp.arange(n_col)[:, None] ^ place[1], jnp.arange(n_row)[None] ^ place[0]
        parts = stacked[row, (col % 2) * (n_col // 2) + col // 2]
        parts = [parts.transpose(0, 1, 3, 2, 4).reshape(order, n_row * width)]
    return pl.pallas_call(
        functools.partial(solve_kernel, n_row, n_col, piece, step),
        out_shape=pltpu.VMEM((order, n_row * width), factor.dtype),
        in_specs=[SMEM, VMEM, VMEM] + [VMEM] * len(parts),
        out_specs=VMEM,
        scratch_shapes=[pltpu.VMEM((order, n_row * width), factor.dtype)],
        compiler_params=room(24),
    )(place, near(factor), near(turned), *map(near, parts))


def strip(ref, a, n_row, n_col):
    if ref.shape[0] == n_col:
        return ref[a]
    return jnp.concatenate([ref[n * n_col + a] for n in range(n_row)], axis=0)


def gram_of(n_row, n_col, a, strips, turned):
    left = jnp.concatenate([strip(ref, a, n_row, n_col) for ref in strips], axis=0)
    return lax.dot_general(
        left, turned[...], (((0,), (0,)), ((), ())), preferred_element_type=jnp.float32
    )


def turn_rows(n_row, piece, masks, place_ref, both_ref, turned):
    if piece % 16:
        turned[...] = both_ref[...]
        return
    row, col = place_ref[0], place_ref[1]
    for i, m in enumerate(masks):
        for n in range(n_row):
            start = ((col ^ m) * n_row + (row ^ n)) * piece
            rows = pl.ds(pl.multiple_of(start, piece), piece)
            there = (i * n_row + n) * piece
            turned[there : there + piece] = both_ref[rows]


def gram_kernel(n_row, n_col, piece, masks, place_ref, both_ref, *refs):
    strips, before, (out, turned) = refs[: len(masks)], refs[len(masks) : -2], refs[-2:]
    turn_rows(n_row, piece, masks, place_ref, both_ref, turned)
    for a in range(n_col):
        gram = gram_of(n_row, n_col, a, strips, turned)
        out[a] = gram + before[0][a] if before else gram


def gram_last_kernel(n_row, n_col, piece, masks, place_ref, map_ref, both_ref, first_ref, cores_ref, *refs):
    strips, chunks = refs[: len(masks)], refs[len(masks) : len(masks) + n_col]
    out, turned, table = refs[-3:]
    row, col = place_ref[0], place_ref[1]
    width = cores_ref.shape[-1]
    turn_rows(n_row, piece, masks, place_ref, both_ref, turned)
    for m in range(n_col):
        for n in range(n_row):
            rank = chunks[m][n_row * n_col, n : n + 1].astype(jnp.float32)
            table[m * n_row + n] = jnp.broadcast_to(rank, table.shape[1:])
    down = lax.broadcasted_iota(jnp.int32, (width, width), 0).astype(jnp.float32)
    across = lax.broadcasted_iota(jnp.int32, (width, width), 1).astype(jnp.float32)

    def rank_of(grid_index):
        owner = map_ref[grid_index]
        entry = ((owner % n_col) ^ col) * n_row + ((owner // n_col) ^ row)
        return table[entry][:1]

    for a in range(n_col):
        gram = gram_of(n_row, n_col, a, strips, turned) + first_ref[a]
        deep = down < rank_of(row * n_col + a)
        for b in range(n_row):
            keep = deep & (across < rank_of(b * n_col + col))
            tile = gram[:, b * width : (b + 1) * width]
            out[a, b] = cores_ref[a, b] - jnp.where(keep, tile, 0.0)


def gram_update(place, owner_map, both, cores, chunks, n_row, n_col, piece):
    order, total = both.shape
    width = cores.shape[-1]
    strips = chunks
    whole = both.reshape(n_col, n_row, piece, total)
    if piece % 16:
        strips = [
            chunk[:-1].reshape(n_row, n_col, piece, width).transpose(1, 0, 2, 3).reshape(n_col, -1, width)
            for chunk in chunks
        ]

    def rows_for(masks):
        if piece % 16 == 0:
            return both
        there = jnp.asarray(masks)[:, None] ^ place[1], jnp.arange(n_row)[None] ^ place[0]
        return whole[there].reshape(-1, total)

    height = order // n_col

    def some(masks, before):
        return pl.pallas_call(
            functools.partial(gram_kernel, n_row, n_col, piece, masks),
            out_shape=pltpu.VMEM((n_col, width, total), jnp.float32),
            in_specs=[SMEM] + [VMEM] * (1 + len(masks) + len(before)),
            out_specs=VMEM,
            scratch_shapes=[pltpu.VMEM((len(masks) * height, total), both.dtype)],
            compiler_params=room(16),
        )(place, near(rows_for(masks)), *[near(strips[m]) for m in masks], *map(near, before))

    first = some(tuple(range(n_col - 2)), [])
    first = some((n_col - 2,), [first])
    cut = n_col - 1
    return pl.pallas_call(
        functools.partial(gram_last_kernel, n_row, n_col, piece, tuple(range(cut, n_col))),
        out_shape=jax.ShapeDtypeStruct(cores.shape, cores.dtype),
        in_specs=[SMEM, SMEM] + [VMEM] * (3 + n_col - cut + n_col),
        out_specs=VMEM,
        scratch_shapes=[
            pltpu.VMEM(((n_col - cut) * height, total), both.dtype),
            pltpu.VMEM((n_row * n_col, 8, width), jnp.float32),
        ],
        compiler_params=room(24),
    )(place, owner_map, near(rows_for(range(cut, n_col))), near(first), cores, *map(near, strips[cut:]), *map(near, chunks))


def panel_step(panel_right, factor_inverse, ranks, owner_map, cores):
    n_row = lax.axis_size("row")
    n_col = lax.axis_size("col")
    blocks, rows, width = panel_right.shape
    piece = rows // n_row
    row = lax.axis_index("row")
    col = lax.axis_index("col")
    place = jnp.stack([row, col]).astype(jnp.int32)
    planes = n_col // 2

    *parts, owner_map = split_rows(
        place, ranks, owner_map, panel_right.reshape(blocks, n_row, piece, width)
    )
    parts = [parts[0]] + [swap(parts[m], "row", m) for m in range(1, n_row)]
    row_parts, col_parts, rank_rows = reorder(place, owner_map, parts, n_row, n_col)

    col_parts = [col_parts[0]] + [swap(col_parts[q], "col", 2 * q) for q in range(1, planes)]
    row_parts = [row_parts[0]] + [swap(row_parts[m], "row", m) for m in range(1, n_row)]
    order = factor_inverse.shape[0]
    step = 256 if order % 256 == 0 else order
    factor, turned = fetch(factor_inverse, step)

    mine = jnp.stack([part[0] for part in col_parts])
    theirs = swap(jnp.stack([part[1] for part in col_parts]), "col", 1)
    row_set = hypercube(jnp.concatenate(row_parts + [rank_rows]), "col", planes, 2)
    col_set = two_way_hypercube(jnp.stack([mine, theirs]), "row", n_row)
    chunks = []
    for part in row_set:
        chunks += [part, swap(part, "col", 1)]

    both = solve(place, factor, turned, col_set, n_row, n_col, piece, step)
    return gram_update(place, owner_map, both, cores[0, 0], chunks, n_row, n_col, piece)[None, None]


def solution(mesh):
    return jax.shard_map(
        panel_step,
        mesh=mesh,
        in_specs=(
            P("row", "col", None),
            P(),
            P(("row", "col")),
            P(),
            P("row", "col", None, None, None, None),
        ),
        out_specs=P("row", "col", None, None, None, None),
        check_vma=False,
    )
```
